32 devices in a mesh: rows: 8 (over y, x, core), cols: 4 (over z).
Axes of the slice: x: 2, y: 2, z: 4, core: 2. Of those that a mesh axis runs over, the one named last changes fastest.
Arguments:
- block_inputs: bfloat16 [64, 128, 384], P('rows', 'cols'), may hold values from -12 to 12
- upstream_adjoint: bfloat16 [64, 128, 384], P('rows', 'cols'), may hold values from -12 to 12
- norm_factor: float32 [384], replicated, may hold values from 0.1 to 1.9
- triple_projection: bfloat16 [384, 1152], replicated, may hold values from -0.3125 to 0.3125
- spatial_filter_taps: bfloat16 [3, 3, 1152], replicated, may hold values from -2 to 2
- sharpness_factors: float32 [8], replicated, may hold values from 4 to 24
- final_projection: bfloat16 [384, 384], replicated, may hold values from -0.3125 to 0.3125
Outputs:
- inputs_adjoint: bfloat16 [64, 128, 384], P('rows', 'cols')
- norm_factor_adjoint: float32 [384], replicated
- spatial_filter_adjoint: float32 [3, 3, 1152], replicated
- sharpness_adjoint: float32 [8], replicated
The draws below stay inside these ranges and needn't reach their ends.
All inputs are finite; a program needn't handle non-finite values.
Results may differ from the reference program's by a relative error of at most 0.0048.
Values may be sent and summed in bfloat16 or wider, within the bound.
A program may use at most 64 MiB of HBM per device.

```python
import math
import jax
import jax.numpy as jnp
from jax import lax

EMBED_WIDTH = 384
FOCUS_GROUPS = 8
NH = 64
NW = 128
PIXEL_TOTAL = 8192


def shared_noise(key):
    noise_key, direction_key = jax.random.split(jax.random.fold_in(key, 11), 2)
    noise = jax.random.normal(noise_key, (NH, NW, EMBED_WIDTH), jnp.float32)
    return (noise, direction_key)


def draw_block_inputs(key, part):
    noise, direction_key = shared_noise(key)
    height = jnp.arange(NH, dtype=jnp.float32) / NH
    across = jnp.arange(NW, dtype=jnp.float32) / NW
    field = 3.0 * height[:, None] + 0.5 * across[None, :]
    direction = jax.random.normal(direction_key, (EMBED_WIDTH,), jnp.float32)
    return jnp.clip(noise + field[:, :, None] * direction[None, None, :], -12.0, 12.0).astype(jnp.bfloat16)


def draw_upstream_adjoint(key, part):
    common, unused_key = shared_noise(key)
    fresh_key = jax.random.fold_in(key, 23)
    height = jnp.arange(NH, dtype=jnp.float32) / NH
    across = jnp.arange(NW, dtype=jnp.float32) / NW
    fresh = jax.random.normal(fresh_key, (NH, NW, EMBED_WIDTH), jnp.float32)
    profile = 0.5 + 1.5 * height[:, None] + 0.0 * across[None, :]
    mixed_noise = 0.6 * common + 0.8 * fresh
    return jnp.clip(profile[:, :, None] * mixed_noise, -12.0, 12.0).astype(jnp.bfloat16)


def scatter_about(rng, extent, scale, bound, kind=jnp.bfloat16):
    return jnp.clip(scale * jax.random.normal(rng, extent, jnp.float32), -bound, bound).astype(kind)


def setup_inputs(seed: int = 0) -> dict:
    streams_of = jax.random.split(jax.random.key(seed), 8)
    return {
        "block_inputs": draw_block_inputs(jax.random.fold_in(streams_of[7], 71), 0),
        "upstream_adjoint": draw_upstream_adjoint(jax.random.fold_in(streams_of[7], 71), 0),
        "norm_factor": jnp.clip(1.0 + 0.18 * jax.random.normal(streams_of[2], (EMBED_WIDTH,), jnp.float32), 0.1, 1.9),
        "triple_projection": scatter_about(streams_of[3], (EMBED_WIDTH, 3 * EMBED_WIDTH), EMBED_WIDTH ** -0.5, 0.3125),
        "spatial_filter_taps": scatter_about(streams_of[4], (3, 3, 3 * EMBED_WIDTH), 9 ** -0.5, 2.0),
        "sharpness_factors": jnp.clip(jnp.exp(jax.random.uniform(streams_of[5], (FOCUS_GROUPS,), jnp.float32, math.log(4.0), math.log(24.0))), 4.0, 24.0),
        "final_projection": scatter_about(streams_of[6], (EMBED_WIDTH, EMBED_WIDTH), EMBED_WIDTH ** -0.5, 0.3125),
    }


norm_eps = 1e-05
unit_eps = 1e-06

def conv_forward(padded, taps):
    total = jnp.zeros((NH, NW, padded.shape[2]), jnp.float32)
    for tap_row in range(3):
        for tap_col in range(3):
            total = total + taps[tap_row, tap_col] * padded[tap_row:tap_row + NH, tap_col:tap_col + NW]
    return total

def conv_backward(padded, taps):
    total = jnp.zeros((NH, NW, padded.shape[2]), jnp.float32)
    for tap_row in range(3):
        for tap_col in range(3):
            total = total + taps[tap_row, tap_col] * padded[2 - tap_row:2 - tap_row + NH, 2 - tap_col:2 - tap_col + NW]
    return total

def reference(block_inputs, upstream_adjoint, norm_factor, triple_projection, spatial_filter_taps, sharpness_factors, final_projection):
    head_size = EMBED_WIDTH // FOCUS_GROUPS
    highest = lax.Precision.HIGHEST
    feat_f = block_inputs.astype(jnp.float32)
    centred = feat_f - lax.optimization_barrier(jnp.mean(feat_f, axis=-1, keepdims=True))
    inv_std = lax.rsqrt(lax.optimization_barrier(jnp.mean(centred * centred, axis=-1, keepdims=True)) + norm_eps)
    standard = centred * inv_std
    normed = (standard * norm_factor).astype(jnp.bfloat16).reshape(PIXEL_TOTAL, EMBED_WIDTH)
    cot_flat = upstream_adjoint.reshape(PIXEL_TOTAL, EMBED_WIDTH)

    def lone_group(grad_acc, group_ordinal):
        start = (group_ordinal * head_size).astype(jnp.int32)
        weight_head = jnp.concatenate([lax.dynamic_slice_in_dim(triple_projection, start + part * EMBED_WIDTH, head_size, 1) for part in range(3)], axis=1)
        taps_head = jnp.concatenate([lax.dynamic_slice_in_dim(spatial_filter_taps, start + part * EMBED_WIDTH, head_size, 2) for part in range(3)], axis=2).astype(jnp.float32)
        qkv_head = jnp.dot(normed, weight_head, preferred_element_type=jnp.float32).astype(jnp.bfloat16)
        padded = jnp.pad(qkv_head.reshape(NH, NW, 3 * head_size), ((1, 1), (1, 1), (0, 0))).astype(jnp.float32)
        convolved = conv_forward(padded, taps_head).reshape(PIXEL_TOTAL, 3 * head_size)
        queries = convolved[:, :head_size]
        keys_part = convolved[:, head_size:2 * head_size]
        values = convolved[:, 2 * head_size:]
        query_scale = lax.rsqrt(lax.optimization_barrier(jnp.sum(queries * queries, axis=0)) + unit_eps)
        keys_scale = lax.rsqrt(lax.optimization_barrier(jnp.sum(keys_part * keys_part, axis=0)) + unit_eps)
        query_unit = queries * query_scale
        keys_unit = keys_part * keys_scale
        similarity_table = jnp.dot(query_unit.T, keys_unit, precision=highest)
        exponent_probs = jnp.exp(sharpness_factors[group_ordinal] * similarity_table)
        attention = exponent_probs / lax.optimization_barrier(jnp.sum(exponent_probs, axis=-1, keepdims=True))
        out_rows = lax.dynamic_slice_in_dim(final_projection, start, head_size, 0)
        grad_out = jnp.dot(cot_flat, out_rows.T, preferred_element_type=jnp.float32)
        grad_attention = jnp.dot(grad_out.T, values, precision=highest)
        grad_values = jnp.dot(grad_out, attention, precision=highest)
        logits_adjoint = attention * (grad_attention - lax.optimization_barrier(jnp.sum(attention * grad_attention, axis=-1, keepdims=True)))
        grad_temp = jnp.sum(logits_adjoint * similarity_table) / PIXEL_TOTAL
        similarity_adjoint = sharpness_factors[group_ordinal] * logits_adjoint
        grad_qunit = jnp.dot(keys_unit, similarity_adjoint.T, precision=highest)
        grad_kunit = jnp.dot(query_unit, similarity_adjoint, precision=highest)
        query_dots = lax.optimization_barrier(jnp.sum(query_unit * grad_qunit, axis=0))
        keys_dots = lax.optimization_barrier(jnp.sum(keys_unit * grad_kunit, axis=0))
        grad_query = query_scale * (grad_qunit - query_unit * query_dots)
        grad_keys = keys_scale * (grad_kunit - keys_unit * keys_dots)
        grad_mixed = jnp.concatenate([grad_query, grad_keys, grad_values], axis=1).astype(jnp.bfloat16)
        grad_mixed_f = grad_mixed.reshape(NH, NW, 3 * head_size).astype(jnp.float32)
        kernel_rows = []
        for tap_row in range(3):
            kernel_cols = []
            for tap_col in range(3):
                kernel_cols.append(lax.optimization_barrier(jnp.sum(padded[tap_row:tap_row + NH, tap_col:tap_col + NW] * grad_mixed_f, axis=(0, 1))))
            kernel_rows.append(jnp.stack(kernel_cols))
        kernel_grad = jnp.stack(kernel_rows) / PIXEL_TOTAL
        grad_padded = jnp.pad(grad_mixed_f, ((1, 1), (1, 1), (0, 0)))
        grad_qkv = conv_backward(grad_padded, taps_head).astype(jnp.bfloat16).reshape(PIXEL_TOTAL, 3 * head_size)
        contrib = jnp.dot(grad_qkv, weight_head.T, preferred_element_type=jnp.float32)
        return (grad_acc + contrib, (kernel_grad, grad_temp))
    standardized_adjoint, (group_filter, sharpness_adjoint) = lax.scan(lone_group, jnp.zeros((PIXEL_TOTAL, EMBED_WIDTH), jnp.float32), jnp.arange(FOCUS_GROUPS, dtype=jnp.int32))
    group_filter = group_filter.reshape(FOCUS_GROUPS, 3, 3, 3, head_size)
    spatial_filter_adjoint = jnp.transpose(group_filter, (1, 2, 3, 0, 4)).reshape(3, 3, 3 * EMBED_WIDTH)
    standard_flat = standard.reshape(PIXEL_TOTAL, EMBED_WIDTH)
    norm_factor_adjoint = lax.optimization_barrier(jnp.sum(standardized_adjoint * standard_flat, axis=0)) / PIXEL_TOTAL
    scaled = standardized_adjoint * norm_factor
    grad_input = inv_std.reshape(PIXEL_TOTAL, 1) * (scaled - lax.optimization_barrier(jnp.mean(scaled, axis=-1, keepdims=True)) - standard_flat * lax.optimization_barrier(jnp.mean(scaled * standard_flat, axis=-1, keepdims=True)))
    inputs_adjoint = (cot_flat.astype(jnp.float32) + grad_input).astype(jnp.bfloat16).reshape(NH, NW, EMBED_WIDTH)
    return (inputs_adjoint, norm_factor_adjoint, spatial_filter_adjoint, sharpness_adjoint)
```

```python
import functools

import jax
import jax.numpy as jnp
from jax import lax
from jax.experimental import pallas as pl
from jax.experimental.pallas import tpu as pltpu
from jax.sharding import PartitionSpec as P

norm_eps = 1e-05
unit_eps = 1e-06
HIGHEST = lax.Precision.HIGHEST
F32 = jnp.float32
BF16 = jnp.bfloat16
LANES = 128


def dot_exact(a, b, dims=((1,), (0,))):
    return lax.dot_general(a, b, (dims, ((), ())), precision=HIGHEST, preferred_element_type=F32)


def dot_bf16(a, b, dims=((1,), (0,))):
    return lax.dot_general(a, b, (dims, ((), ())), preferred_element_type=F32)


def ceil_to(value, step):
    return (value + step - 1) // step * step


def kernel(
    geo,
    x_ref,
    u_ref,
    gain_ref,
    proj_ref,
    taps_ref,
    sharp_ref,
    final_ref,
    out_ref,
    gain_out,
    taps_out,
    sharp_out,
    stage,
    col_in,
    corner_in,
    row_x,
    row_u,
    xe,
    ue,
    standard_ref,
    inv_ref,
    qkv,
    mixed,
    grad_out,
    grad_mixed,
    grad_qkv,
    pay1,
    part1,
    cols1,
    full1,
    pay2,
    part2,
    cols2,
    full2,
    halo_send,
    halo_recv,
    scatter_send,
    scatter_recv,
    cols_send,
    cols_recv,
    gather_send,
    gather_recv,
):
    R, C, H, B, ch, heads = geo
    hd = ch // heads
    c3 = 3 * ch
    W = B + 8
    row = lax.axis_index("rows")
    col = lax.axis_index("cols")
    up, down = lax.rem(row + R - 1, R), lax.rem(row + 1, R)
    left, right = lax.rem(col + C - 1, C), lax.rem(col + 1, C)
    MESH = pl.DeviceIdType.MESH

    barrier = pltpu.get_barrier_semaphore()

    def greet(r, c):
        pl.semaphore_signal(barrier, inc=1, device_id=(r, c), device_id_type=MESH)

    @pl.loop(1, R)
    def _(i):
        greet(lax.rem(row + i, R), col)

    @pl.loop(1, C)
    def _(i):
        greet(row, lax.rem(col + i, C))

    for r in (up, down):
        for c in (left, right):
            greet(r, c)

    xf = x_ref[...].astype(F32)
    uf = u_ref[...].astype(F32)
    stage[0, :, 0:2, :] = xf[:, 0:2, :]
    stage[0, :, 2:3, :] = uf[:, 0:1, :]
    stage[0, :, 3:4, :] = uf[:, 0:1, :]
    stage[1, :, 0:2, :] = xf[:, B - 2 : B, :]
    stage[1, :, 2:3, :] = uf[:, B - 1 : B, :]
    stage[1, :, 3:4, :] = uf[:, B - 1 : B, :]

    pl.semaphore_wait(barrier, (R - 1) + (C - 1) + 4)

    def send(n, src, dst, r, c):
        copy = pltpu.make_async_remote_copy(
            src_ref=src,
            dst_ref=dst,
            send_sem=halo_send.at[n],
            recv_sem=halo_recv.at[n],
            device_id=(r, c),
            device_id_type=MESH,
        )
        copy.start()
        return copy

    copies = [
        send(0, stage.at[0], col_in.at[1], row, left),
        send(1, stage.at[1], col_in.at[0], row, right),
        send(2, x_ref.at[pl.ds(0, 2)], row_x.at[1], up, col),
        send(3, x_ref.at[pl.ds(H - 2, 2)], row_x.at[0], down, col),
        send(4, u_ref.at[pl.ds(0, 1)], row_u.at[1], up, col),
        send(5, u_ref.at[pl.ds(H - 1, 1)], row_u.at[0], down, col),
        send(6, stage.at[0, pl.ds(0, 2)], corner_in.at[1, 1], up, left),
        send(7, stage.at[1, pl.ds(0, 2)], corner_in.at[1, 0], up, right),
        send(8, stage.at[0, pl.ds(H - 2, 2)], corner_in.at[0, 1], down, left),
        send(9, stage.at[1, pl.ds(H - 2, 2)], corner_in.at[0, 0], down, right),
    ]

    xe[2 : H + 2, 0:B, :] = xf
    xe[:, B:W, :] = jnp.zeros((H + 4, W - B, ch), F32)
    ue[1 : H + 1, 0:B, :] = uf
    ue[:, B:W, :] = jnp.zeros((H + 2, W - B, ch), F32)
    for copy in copies:
        copy.wait()
    xe[2 : H + 2, B : B + 2, :] = col_in[1, :, 0:2, :]
    xe[2 : H + 2, W - 2 : W, :] = col_in[0, :, 0:2, :]
    ue[1 : H + 1, B : B + 1, :] = col_in[1, :, 2:3, :]
    ue[1 : H + 1, W - 1 : W, :] = col_in[0, :, 2:3, :]
    for v, at in ((0, 0), (1, H + 2)):
        xe[at : at + 2, 0:B, :] = row_x[v].astype(F32)
        xe[at : at + 2, B : B + 2, :] = corner_in[v, 1, :, 0:2, :]
        xe[at : at + 2, W - 2 : W, :] = corner_in[v, 0, :, 0:2, :]
    for v, at, near in ((0, 0, 1), (1, H + 1, 0)):
        ue[at : at + 1, 0:B, :] = row_u[v].astype(F32)
        ue[at : at + 1, B : B + 1, :] = corner_in[v, 1, near : near + 1, 2:3, :]
        ue[at : at + 1, W - 1 : W, :] = corner_in[v, 0, near : near + 1, 2:3, :]

    def inside(width):
        shape = (H + 2 * width, W, LANES)
        i = row * H - width + lax.broadcasted_iota(jnp.int32, shape, 0)
        j = lax.broadcasted_iota(jnp.int32, shape, 1)
        near = j < B
        rim_right = (j >= B) & (j < B + width) & (col < C - 1)
        rim_left = (j >= W - width) & (col > 0)
        ok = (i >= 0) & (i < R * H) & (near | rim_right | rim_left)
        return jnp.where(ok, 1.0, 0.0).astype(F32)

    n2 = (H + 4) * W
    n1 = (H + 2) * W
    n0 = H * B
    feat = xe[...].reshape(n2, ch)
    centred = feat - jnp.mean(feat, axis=-1, keepdims=True)
    inv_std = lax.rsqrt(jnp.mean(centred * centred, axis=-1, keepdims=True) + norm_eps)
    standard = centred * inv_std
    standard_ref[...] = standard.reshape(H + 4, W, ch)[2 : H + 2, 0:B, :].reshape(n0, ch)
    inv_ref[...] = jnp.broadcast_to(
        inv_std.reshape(H + 4, W, 1)[2 : H + 2, 0:B, :].reshape(n0, 1), (n0, LANES)
    )
    mask2 = inside(2).reshape(n2, LANES)[:, 0:1] > 0.5
    normed = jnp.where(mask2, standard * gain_ref[...], 0.0).astype(BF16)
    qkv[...] = dot_bf16(normed, proj_ref[...]).astype(BF16).astype(F32).reshape(H + 4, W, c3)
    mask1 = inside(1).reshape(n1, LANES)[:, 0:1] > 0.5
    adjoint = jnp.where(mask1, ue[...].reshape(n1, ch), 0.0).astype(BF16)
    grad_out[...] = dot_bf16(adjoint, final_ref[...], ((1,), (1,)))

    def tap_rows(lanes):
        return [
            [taps_ref[a, :, lanes].astype(F32)[b : b + 1, :] for b in range(3)] for a in range(3)
        ]

    @pl.loop(0, c3 // LANES)
    def _(n):
        lanes = pl.ds(pl.multiple_of(n * LANES, LANES), LANES)
        taps = tap_rows(lanes)

        @pl.loop(0, H + 2)
        def _(i):
            window = [qkv[i + a, :, lanes] for a in range(3)]
            t = [sum(taps[a][b] * window[a] for a in range(3)) for b in range(3)]
            mixed[i, :, lanes] = t[1] + pltpu.roll(t[0], 1, 0) + pltpu.roll(t[2], W - 1, 0)

    def own(lo):
        return mixed[1 : H + 1, 0:B, lo : lo + ch].reshape(n0, ch)

    q, k, v = own(0), own(ch), own(2 * ch)
    g = grad_out[...].reshape(H + 2, W, ch)[1 : H + 1, 0:B, :].reshape(n0, ch)
    head_r = lax.broadcasted_iota(jnp.int32, (ch, ch), 0) // hd
    head_c = lax.broadcasted_iota(jnp.int32, (ch, ch), 1) // hd
    same_head = head_r == head_c
    along = ((0,), (0,))
    raw_gram = jnp.where(same_head, dot_exact(q, k, along), 0.0)
    raw_attn = jnp.where(same_head, dot_exact(g, v, along), 0.0)
    ones = jnp.ones((n0, LANES), F32)
    q_squares = dot_exact(q * q, ones, along)
    k_squares = dot_exact(k * k, ones, along)
    place_r = lax.rem(lax.broadcasted_iota(jnp.int32, (ch, LANES), 0), hd)
    place_c = lax.broadcasted_iota(jnp.int32, (ch, LANES), 1)
    fold_a = jnp.where(place_r == place_c, 1.0, 0.0).astype(F32)
    fold_b = jnp.where(place_r + hd == place_c, 1.0, 0.0).astype(F32)
    packed = dot_exact(raw_gram, fold_a) + dot_exact(raw_attn, fold_b)
    packed = jnp.where(place_c == 2 * hd, q_squares, packed)
    packed = jnp.where(place_c == 2 * hd + 1, k_squares, packed)
    size1 = pay1.shape[1]
    pay1[...] = pay_rows(packed, R * size1).reshape(R, size1, LANES)

    def reduce_all(stage_no, pay, part, cols, full):
        def rs(i):
            to = lax.rem(row + i, R)
            return pltpu.make_async_remote_copy(
                src_ref=pay.at[to],
                dst_ref=part.at[row],
                send_sem=scatter_send.at[stage_no, to],
                recv_sem=scatter_recv.at[stage_no, row],
                device_id=(to, col),
                device_id_type=MESH,
            )

        def rs_in(i):
            source = lax.rem(row + i, R)
            return pltpu.make_async_remote_copy(
                src_ref=pay.at[source],
                dst_ref=part.at[source],
                send_sem=scatter_send.at[stage_no, source],
                recv_sem=scatter_recv.at[stage_no, source],
                device_id=(source, col),
                device_id_type=MESH,
            )

        @pl.loop(1, R)
        def _(i):
            rs(i).start()

        part[row] = pay[row]

        @pl.loop(1, R)
        def _(i):
            rs_in(i).wait()

        total = part[0]
        for i in range(1, R):
            total = total + part[i]
        cols[col] = total

        def cs(i):
            to = lax.rem(col + i, C)
            return pltpu.make_async_remote_copy(
                src_ref=cols.at[col],
                dst_ref=cols.at[col],
                send_sem=cols_send.at[stage_no, to],
                recv_sem=cols_recv.at[stage_no, col],
                device_id=(row, to),
                device_id_type=MESH,
            )

        def cs_in(i):
            source = lax.rem(col + i, C)
            return pltpu.make_async_remote_copy(
                src_ref=cols.at[source],
                dst_ref=cols.at[source],
                send_sem=cols_send.at[stage_no, source],
                recv_sem=cols_recv.at[stage_no, source],
                device_id=(row, source),
                device_id_type=MESH,
            )

        @pl.loop(1, C)
        def _(i):
            cs(i).start()

        @pl.loop(1, C)
        def _(i):
            cs_in(i).wait()

        total = cols[0]
        for i in range(1, C):
            total = total + cols[i]
        full[row] = total

        def ag(i):
            to = lax.rem(row + i, R)
            return pltpu.make_async_remote_copy(
                src_ref=full.at[row],
                dst_ref=full.at[row],
                send_sem=gather_send.at[stage_no, to],
                recv_sem=gather_recv.at[stage_no, row],
                device_id=(to, col),
                device_id_type=MESH,
            )

        def ag_in(i):
            source = lax.rem(row + i, R)
            return pltpu.make_async_remote_copy(
                src_ref=full.at[source],
                dst_ref=full.at[source],
                send_sem=gather_send.at[stage_no, source],
                recv_sem=gather_recv.at[stage_no, source],
                device_id=(source, col),
                device_id_type=MESH,
            )

        @pl.loop(1, R)
        def _(i):
            ag(i).start()

        @pl.loop(1, R)
        def _(i):
            ag_in(i).wait()

    reduce_all(0, pay1, part1, cols1, full1)

    packed = full1[...].reshape(R * size1, LANES)[0:ch, :]
    q_scale = lax.rsqrt(packed[:, 2 * hd : 2 * hd + 1] + unit_eps)
    k_scale = lax.rsqrt(packed[:, 2 * hd + 1 : 2 * hd + 2] + unit_eps)
    diagonal = lax.broadcasted_iota(jnp.int32, (ch, ch), 0) == lax.broadcasted_iota(
        jnp.int32, (ch, ch), 1
    )

    def as_row(column):
        return jnp.sum(jnp.where(diagonal, column, 0.0), axis=0, keepdims=True)

    q_scale_row, k_scale_row = as_row(q_scale), as_row(k_scale)
    across = ((1,), (1,))
    gram = jnp.where(same_head, dot_exact(packed, fold_a, across), 0.0) * q_scale * k_scale_row
    grad_attn = jnp.where(same_head, dot_exact(packed, fold_b, across), 0.0)
    head_of = lax.broadcasted_iota(jnp.int32, (ch, 1), 0) // hd
    sharp = jnp.zeros((ch, 1), F32)
    for h in range(heads):
        sharp = jnp.where(head_of == h, sharp_ref[h], sharp)
    powers = jnp.where(same_head, jnp.exp(sharp * gram), 0.0)
    attention = powers / jnp.sum(powers, axis=-1, keepdims=True)
    scores = attention * (grad_attn - jnp.sum(attention * grad_attn, axis=-1, keepdims=True))
    pixels = R * C * n0
    per_channel = jnp.sum(scores * gram, axis=-1, keepdims=True)
    lane_head = lax.broadcasted_iota(jnp.int32, (ch, LANES), 1)
    row_head = lax.broadcasted_iota(jnp.int32, (ch, LANES), 0) // hd
    sharp_out[...] = (
        jnp.sum(jnp.where(lane_head == row_head, per_channel, 0.0), axis=0, keepdims=True) / pixels
    )
    grad_gram = sharp * scores
    q_dots = as_row(jnp.sum(grad_gram * gram, axis=-1, keepdims=True))
    k_dots = jnp.sum(grad_gram * gram, axis=0, keepdims=True)
    blend = q_scale * grad_gram * k_scale_row

    q_wide = mixed[:, :, 0:ch].reshape(n1, ch)
    k_wide = mixed[:, :, ch : 2 * ch].reshape(n1, ch)

    def keep(value, lo):
        value = jnp.where(mask1, value, 0.0).astype(BF16).astype(F32)
        grad_mixed[:, :, lo : lo + ch] = value.reshape(H + 2, W, ch)

    keep(dot_exact(k_wide, blend, across) - q_wide * (q_scale_row * q_scale_row * q_dots), 0)
    keep(dot_exact(q_wide, blend) - k_wide * (k_scale_row * k_scale_row * k_dots), ch)
    keep(dot_exact(grad_out[...], attention), 2 * ch)

    size2 = pay2.shape[0] // R
    pay2[...] = jnp.zeros_like(pay2)
    own_cols = lax.broadcasted_iota(jnp.int32, (W, LANES), 0) < B
    strips = W // 8

    @pl.loop(0, c3 // LANES)
    def _(n):
        lanes = pl.ds(pl.multiple_of(n * LANES, LANES), LANES)
        taps = tap_rows(lanes)

        def body(i, sums):
            grads = [grad_mixed[i + 2 - a, :, lanes] for a in range(3)]
            s = [sum(taps[a][b] * grads[a] for a in range(3)) for b in range(3)]
            value = s[1] + pltpu.roll(s[0], W - 1, 0) + pltpu.roll(s[2], 1, 0)
            grad_qkv[i, :, lanes] = value[0:B, :].astype(BF16)
            mid = jnp.where(own_cols, grads[1], 0.0)
            moved = [pltpu.roll(mid, W - 1, 0), mid, pltpu.roll(mid, 1, 0)]
            new = []
            for a in range(3):
                window = qkv[i + 1 + a, :, lanes]
                for b in range(3):
                    term = (window * moved[b]).reshape(strips, 8, LANES)
                    new.append(sums[3 * a + b] + jnp.sum(term, axis=0))
            return tuple(new)

        sums = lax.fori_loop(0, H, body, tuple(jnp.zeros((8, LANES), F32) for _ in range(9)))
        for t in range(9):
            pay2[pl.ds(n * 9 + t, 1), :] = jnp.sum(sums[t], axis=0, keepdims=True)

    grad_normed = dot_bf16(grad_qkv[...].reshape(n0, c3), proj_ref[...], across)
    standard = standard_ref[...]
    product = grad_normed * standard
    gain_sum = jnp.sum(product, axis=0, keepdims=True)
    base = 9 * (c3 // LANES)
    for n in range(ch // LANES):
        pay2[base + n : base + n + 1, :] = gain_sum[:, n * LANES : (n + 1) * LANES]
    scaled = grad_normed * gain_ref[...]
    slope = jnp.mean(scaled * standard, axis=-1, keepdims=True)
    grad_input = inv_ref[:, 0:1] * (
        scaled - jnp.mean(scaled, axis=-1, keepdims=True) - standard * slope
    )
    out_ref[...] = (u_ref[...].astype(F32) + grad_input.reshape(H, B, ch)).astype(BF16)

    reduce_all(
        1, pay2.reshape(R, size2, LANES), part2, cols2, full2
    )
    flat = full2[...].reshape(R * size2, LANES) / pixels
    for n in range(c3 // LANES):
        taps_out[:, n * LANES : (n + 1) * LANES] = flat[n * 9 : n * 9 + 9, :]
    for n in range(ch // LANES):
        gain_out[:, n * LANES : (n + 1) * LANES] = flat[base + n : base + n + 1, :]


def pay_rows(value, rows):
    if rows == value.shape[0]:
        return value
    fill = jnp.zeros((rows - value.shape[0], value.shape[1]), value.dtype)
    return jnp.concatenate([value, fill], axis=0)


def local(R, C, x, u, gain, proj, taps, sharp, final):
    H, B, ch = x.shape
    heads = sharp.shape[0]
    c3 = 3 * ch
    W = B + 8
    size1 = ceil_to(-(-ch // R), 8)
    rows2 = 9 * (c3 // LANES) + ch // LANES
    size2 = ceil_to(-(-rows2 // R), 8)
    vmem = pl.BlockSpec(memory_space=pltpu.VMEM)
    DMA = pltpu.SemaphoreType.DMA
    out, gain_sum, taps_sum, sharp_sum = pl.pallas_call(
        functools.partial(kernel, (R, C, H, B, ch, heads)),
        name="attention_backward",
        out_shape=(
            jax.ShapeDtypeStruct((H, B, ch), BF16),
            jax.ShapeDtypeStruct((1, ch), F32),
            jax.ShapeDtypeStruct((9, c3), F32),
            jax.ShapeDtypeStruct((1, LANES), F32),
        ),
        in_specs=[vmem] * 5 + [pl.BlockSpec(memory_space=pltpu.SMEM), vmem],
        out_specs=[vmem] * 4,
        scratch_shapes=[
            pltpu.VMEM((2, H, 4, ch), F32),
            pltpu.VMEM((2, H, 4, ch), F32),
            pltpu.VMEM((2, 2, 2, 4, ch), F32),
            pltpu.VMEM((2, 2, B, ch), BF16),
            pltpu.VMEM((2, 1, B, ch), BF16),
            pltpu.VMEM((H + 4, W, ch), F32),
            pltpu.VMEM((H + 2, W, ch), F32),
            pltpu.VMEM((H * B, ch), F32),
            pltpu.VMEM((H * B, LANES), F32),
            pltpu.VMEM((H + 4, W, c3), F32),
            pltpu.VMEM((H + 2, W, c3), F32),
            pltpu.VMEM(((H + 2) * W, ch), F32),
            pltpu.VMEM((H + 2, W, c3), F32),
            pltpu.VMEM((H, B, c3), BF16),
            pltpu.VMEM((R, size1, LANES), F32),
            pltpu.VMEM((R, size1, LANES), F32),
            pltpu.VMEM((C, size1, LANES), F32),
            pltpu.VMEM((R, size1, LANES), F32),
            pltpu.VMEM((R * size2, LANES), F32),
            pltpu.VMEM((R, size2, LANES), F32),
            pltpu.VMEM((C, size2, LANES), F32),
            pltpu.VMEM((R, size2, LANES), F32),
            DMA((10,)),
            DMA((10,)),
            DMA((2, R)),
            DMA((2, R)),
            DMA((2, C)),
            DMA((2, C)),
            DMA((2, R)),
            DMA((2, R)),
        ],
        compiler_params=pltpu.CompilerParams(
            collective_id=0, has_side_effects=True, vmem_limit_bytes=48 << 20
        ),
    )(x, u, gain.reshape(1, ch), proj, taps, sharp, final)
    return (out, gain_sum.reshape(ch), taps_sum.reshape(3, 3, c3), sharp_sum[0, :heads])


def solution(mesh):
    R, C = mesh.shape["rows"], mesh.shape["cols"]
    return jax.shard_map(
        functools.partial(local, R, C),
        mesh=mesh,
        in_specs=(P("rows", "cols", None), P("rows", "cols", None), P(), P(), P(), P(), P()),
        out_specs=(P("rows", "cols", None), P(), P(), P()),
        check_vma=False,
    )
```

```python
import functools

import jax
import jax.numpy as jnp
from jax import lax
from jax.experimental import pallas as pl
from jax.experimental.pallas import tpu as pltpu
from jax.sharding import PartitionSpec as P

norm_eps = 1e-05
unit_eps = 1e-06
F32 = jnp.float32
BF16 = jnp.bfloat16
LANES = 128


def dot_bf16(a, b, dims=((1,), (0,))):
    return lax.dot_general(a, b, (dims, ((), ())), preferred_element_type=F32)


def ceil_to(value, step):
    return (value + step - 1) // step * step


def halves(a):
    high = a.astype(BF16)
    return high, (a - high.astype(F32)).astype(BF16)


def dot_split(a, b, dims=((1,), (0,))):
    return dot_bf16(a[0], b[0], dims) + (dot_bf16(a[0], b[1], dims) + dot_bf16(a[1], b[0], dims))


def kernel(
    geo,
    x_hbm,
    u_hbm,
    gain_hbm,
    proj_hbm,
    taps_hbm,
    sharp_ref,
    final_hbm,
    out_hbm,
    gain_out,
    taps_out,
    sharp_out,
    x_ref,
    u_ref,
    gain_ref,
    proj_ref,
    taps_ref,
    final_ref,
    out_ref,
    load_sem,
    stage,
    col_in,
    corner_in,
    row_x,
    row_u,
    rim_x,
    side_x,
    rim_u,
    side_u,
    standard_ref,
    inv_ref,
    qkv,
    mixed,
    grad_out,
    grad_mixed,
    grad_qkv,
    split,
    pay1,
    part1,
    cols1,
    full1,
    pay2,
    part2,
    cols2,
    full2,
    gain_all,
    gain_cols,
    halo_send,
    halo_recv,
    red_send,
    red_recv,
):
    R, C, H, B, ch, heads = geo
    hd = ch // heads
    c3 = 3 * ch
    W = B + 8
    S = W - B
    row = lax.axis_index("rows")
    col = lax.axis_index("cols")
    up, down = lax.rem(row + R - 1, R), lax.rem(row + 1, R)
    left, right = lax.rem(col + C - 1, C), lax.rem(col + 1, C)
    MESH = pl.DeviceIdType.MESH

    barrier = pltpu.get_barrier_semaphore()

    def greet(r, c):
        pl.semaphore_signal(barrier, inc=1, device_id=(r, c), device_id_type=MESH)

    for i in range(1, R):
        greet(lax.rem(row + i, R), col)
    for i in range(1, C):
        greet(row, lax.rem(col + i, C))
    for r in (up, down):
        for c in (left, right):
            greet(r, c)

    loads = [
        pltpu.make_async_copy(src, dst, load_sem.at[n])
        for n, (src, dst) in enumerate(
            (
                (x_hbm, x_ref),
                (u_hbm, u_ref),
                (gain_hbm, gain_ref.at[0]),
                (proj_hbm, proj_ref),
                (final_hbm, final_ref),
                (taps_hbm, taps_ref),
            )
        )
    ]
    for load in loads:
        load.start()
    loads[0].wait()
    loads[1].wait()
    xf = x_ref[...].astype(F32)
    uf = u_ref[...].astype(F32)
    stage[0, :, 0:2, :] = xf[:, 0:2, :]
    stage[0, :, 2:3, :] = uf[:, 0:1, :]
    stage[0, :, 3:4, :] = uf[:, 0:1, :]
    stage[1, :, 0:2, :] = xf[:, B - 2 : B, :]
    stage[1, :, 2:3, :] = uf[:, B - 1 : B, :]
    stage[1, :, 3:4, :] = uf[:, B - 1 : B, :]

    pl.semaphore_wait(barrier, (R - 1) + (C - 1) + 4)

    def send(n, src, dst, r, c):
        pltpu.make_async_remote_copy(
            src_ref=src,
            dst_ref=dst,
            send_sem=halo_send.at[n],
            recv_sem=halo_recv.at[n],
            device_id=(r, c),
            device_id_type=MESH,
        ).start()

    send(0, stage.at[0], col_in.at[1], row, left)
    send(0, stage.at[1], col_in.at[0], row, right)
    send(1, stage.at[0, pl.ds(0, 2)], corner_in.at[1, 1], up, left)
    send(1, stage.at[1, pl.ds(0, 2)], corner_in.at[1, 0], up, right)
    send(1, stage.at[0, pl.ds(H - 2, 2)], corner_in.at[0, 1], down, left)
    send(1, stage.at[1, pl.ds(H - 2, 2)], corner_in.at[0, 0], down, right)
    send(2, x_ref.at[pl.ds(0, 2)], row_x.at[1], up, col)
    send(2, x_ref.at[pl.ds(H - 2, 2)], row_x.at[0], down, col)
    send(3, u_ref.at[pl.ds(0, 1)], row_u.at[1], up, col)
    send(3, u_ref.at[pl.ds(H - 1, 1)], row_u.at[0], down, col)

    def halo_copy(n, buf):
        return pltpu.make_async_remote_copy(
            src_ref=buf,
            dst_ref=buf,
            send_sem=halo_send.at[n],
            recv_sem=halo_recv.at[n],
            device_id=(row, left),
            device_id_type=MESH,
        )

    n0 = H * B
    across = ((1,), (1,))

    def normalise(feat):
        centred = feat - jnp.mean(feat, axis=-1, keepdims=True)
        inv_std = lax.rsqrt(jnp.mean(centred * centred, axis=-1, keepdims=True) + norm_eps)
        return centred * inv_std, inv_std

    def project(normed):
        return dot_bf16(normed.astype(BF16), proj_ref[...]).astype(BF16).astype(F32)

    loads[2].wait()
    loads[3].wait()
    standard, inv_std = normalise(xf.reshape(n0, ch))
    standard_ref[...] = standard
    inv_ref[...] = jnp.broadcast_to(inv_std, (n0, LANES))
    qkv[2 : H + 2, 0:B, :] = project(standard * gain_ref[...]).reshape(H, B, c3)
    loads[4].wait()
    loads[5].wait()
    grad_out[1 : H + 1, 0:B, :] = dot_bf16(
        u_ref[...].reshape(n0, ch), final_ref[...], across
    ).reshape(H, B, ch)

    rim_x[:, B:W, :] = jnp.zeros((4, S, ch), F32)
    side_x[...] = jnp.zeros((H, S, ch), F32)
    rim_u[:, B:W, :] = jnp.zeros((2, S, ch), F32)
    side_u[...] = jnp.zeros((H, S, ch), F32)
    halo_copy(0, col_in).wait_recv()
    halo_copy(1, corner_in).wait_recv()
    halo_copy(2, row_x).wait_recv()
    halo_copy(3, row_u).wait_recv()
    side_x[:, 0:2, :] = col_in[1, :, 0:2, :]
    side_x[:, S - 2 : S, :] = col_in[0, :, 0:2, :]
    for v in (0, 1):
        at = 2 * v
        rim_x[at : at + 2, 0:B, :] = row_x[v].astype(F32)
        rim_x[at : at + 2, B : B + 2, :] = corner_in[v, 1, :, 0:2, :]
        rim_x[at : at + 2, W - 2 : W, :] = corner_in[v, 0, :, 0:2, :]

    def inside(shape, i, first_col, width):
        j = first_col + lax.broadcasted_iota(jnp.int32, shape, 1)
        rim_right = (j >= B) & (j < B + width) & (col < C - 1)
        rim_left = (j >= W - width) & (col > 0)
        ok = (i >= 0) & (i < R * H) & ((j < B) | rim_right | rim_left)
        return jnp.where(ok, 1.0, 0.0).astype(F32).reshape(-1, LANES)[:, 0:1] > 0.5

    def plane(shape):
        return lax.broadcasted_iota(jnp.int32, shape, 0)

    n_rim, n_side = 4 * W, H * S
    plane4 = plane((4, W, LANES))
    rim_rows = row * H + jnp.where(plane4 < 2, plane4 - 2, plane4 + H - 2)
    rim_ok = inside((4, W, LANES), rim_rows, 0, 2)
    side_ok = inside((H, S, LANES), row * H + plane((H, S, LANES)), B, 2)
    rim_norm = normalise(rim_x[...].reshape(n_rim, ch))[0] * gain_ref[...]
    side_norm = normalise(side_x[...].reshape(n_side, ch))[0] * gain_ref[...]
    rim_qkv = project(
        jnp.concatenate([jnp.where(rim_ok, rim_norm, 0.0), jnp.where(side_ok, side_norm, 0.0)], 0)
    )
    qkv[0:2, :, :] = rim_qkv[0 : 2 * W].reshape(2, W, c3)
    qkv[H + 2 : H + 4, :, :] = rim_qkv[2 * W : n_rim].reshape(2, W, c3)
    qkv[2 : H + 2, B:W, :] = rim_qkv[n_rim:].reshape(H, S, c3)

    def tap_rows(lanes):
        return [
            [taps_ref[a, :, lanes].astype(F32)[b : b + 1, :] for b in range(3)] for a in range(3)
        ]

    def lanes_of(n):
        return pl.ds(pl.multiple_of(n * LANES, LANES), LANES)

    def mix(taps, lanes, i):
        window = [qkv[i + a, :, lanes] for a in range(3)]
        t = [sum(taps[a][b] * window[a] for a in range(3)) for b in range(3)]
        mixed[i, :, lanes] = t[1] + pltpu.roll(t[0], 1, 0) + pltpu.roll(t[2], W - 1, 0)

    @pl.loop(0, c3 // LANES)
    def _(n):
        taps = tap_rows(lanes_of(n))
        for i in range(1, H + 1):
            mix(taps, lanes_of(n), i)

    def own(lo):
        return mixed[1 : H + 1, 0:B, lo : lo + ch].reshape(n0, ch)

    q, k, v = own(0), own(ch), own(2 * ch)
    g = grad_out[1 : H + 1, 0:B, :].reshape(n0, ch)
    head_r = lax.broadcasted_iota(jnp.int32, (ch, ch), 0) // hd
    head_c = lax.broadcasted_iota(jnp.int32, (ch, ch), 1) // hd
    same_head = head_r == head_c
    diagonal = lax.broadcasted_iota(jnp.int32, (ch, ch), 0) == lax.broadcasted_iota(
        jnp.int32, (ch, ch), 1
    )
    along = ((0,), (0,))

    def as_column(line):
        return jnp.sum(jnp.where(diagonal, line, 0.0), axis=1, keepdims=True)

    def as_row(column):
        return jnp.sum(jnp.where(diagonal, column, 0.0), axis=0, keepdims=True)

    raw_gram = jnp.where(same_head, dot_split(halves(q), halves(k), along), 0.0)
    raw_attn = jnp.where(same_head, dot_split(halves(g), halves(v), along), 0.0)
    q_squares = as_column(jnp.sum(q * q, axis=0, keepdims=True))
    k_squares = as_column(jnp.sum(k * k, axis=0, keepdims=True))
    place_r = lax.rem(lax.broadcasted_iota(jnp.int32, (ch, LANES), 0), hd)
    place_c = lax.broadcasted_iota(jnp.int32, (ch, LANES), 1)
    fold_a = jnp.where(place_r == place_c, 1.0, 0.0).astype(BF16)
    fold_b = jnp.where(place_r + hd == place_c, 1.0, 0.0).astype(BF16)

    def thirds(a):
        high, low = halves(a)
        return high, low, (a - high.astype(F32) - low.astype(F32)).astype(BF16)

    def fold(a, matrix, dims=((1,), (0,))):
        return sum(dot_bf16(part, matrix, dims) for part in thirds(a))

    packed = fold(raw_gram, fold_a) + fold(raw_attn, fold_b)
    packed = jnp.where(place_c == 2 * hd, q_squares, packed)
    packed = jnp.where(place_c == 2 * hd + 1, k_squares, packed)
    size1 = pay1.shape[1]
    pay1[...] = pay_rows(packed, R * size1).reshape(R, size1, LANES)

    def copy_to(phase, src, dst, r, c):
        return pltpu.make_async_remote_copy(
            src_ref=src,
            dst_ref=dst,
            send_sem=red_send.at[phase],
            recv_sem=red_recv.at[phase],
            device_id=(r, c),
            device_id_type=MESH,
        )

    def arrive(phase, buf, count):
        some = buf.at[pl.ds(0, count)]
        copy_to(phase, some, some, row, left).wait_recv()

    def left_here(phase, buf, count):
        some = buf.at[pl.ds(0, count)]
        copy_to(phase, some, some, row, left).wait_send()

    def scatter(phase, pay, part):
        for i in range(1, R):
            to = lax.rem(row + i, R)
            copy_to(phase, pay.at[to], part.at[i - 1], to, col).start()

    def scattered(phase, pay, part):
        arrive(phase, part, R - 1)
        total = pay[row]
        for i in range(R - 1):
            total = total + part[i]
        return total

    def to_cols(phase, cols, value):
        cols[col] = value
        for i in range(1, C):
            to = lax.rem(col + i, C)
            copy_to(phase, cols.at[col], cols.at[col], row, to).start()

    def summed(phase, buf, count):
        arrive(phase, buf, count - 1)
        total = buf[0]
        for i in range(1, count):
            total = total + buf[i]
        return total

    def to_rows(phase, full, value):
        full[row] = value
        for i in range(1, R):
            to = lax.rem(row + i, R)
            copy_to(phase, full.at[row], full.at[row], to, col).start()

    scatter(0, pay1, part1)

    @pl.loop(0, c3 // LANES)
    def _(n):
        taps = tap_rows(lanes_of(n))
        for i in (0, H + 1):
            mix(taps, lanes_of(n), i)

    side_u[:, 0:1, :] = col_in[1, :, 2:3, :]
    side_u[:, S - 1 : S, :] = col_in[0, :, 2:3, :]
    for v, near in ((0, 1), (1, 0)):
        rim_u[v : v + 1, 0:B, :] = row_u[v].astype(F32)
        rim_u[v : v + 1, B : B + 1, :] = corner_in[v, 1, near : near + 1, 2:3, :]
        rim_u[v : v + 1, W - 1 : W, :] = corner_in[v, 0, near : near + 1, 2:3, :]
    n1 = (H + 2) * W
    rows1 = row * H - 1 + plane((H + 2, W, LANES))
    mask1 = inside((H + 2, W, LANES), rows1, 0, 1)
    rim_adjoint = jnp.concatenate(
        [rim_u[...].reshape(2 * W, ch), side_u[...].reshape(n_side, ch)], 0
    ).astype(BF16)
    rim_out = dot_bf16(rim_adjoint, final_ref[...], across)
    grad_out[0:1, :, :] = rim_out[0:W].reshape(1, W, ch)
    grad_out[H + 1 : H + 2, :, :] = rim_out[W : 2 * W].reshape(1, W, ch)
    grad_out[1 : H + 1, B:W, :] = rim_out[2 * W :].reshape(H, S, ch)
    for n, wide in enumerate((mixed[:, :, 0:ch], mixed[:, :, ch : 2 * ch], grad_out[...])):
        split[2 * n], split[2 * n + 1] = halves(wide.reshape(n1, ch))

    to_cols(1, cols1, scattered(0, pay1, part1))
    to_rows(2, full1, summed(1, cols1, C))
    arrive(2, full1, R - 1)

    packed = full1[...].reshape(R * size1, LANES)[0:ch, :]
    q_scale = lax.rsqrt(packed[:, 2 * hd : 2 * hd + 1] + unit_eps)
    k_scale = lax.rsqrt(packed[:, 2 * hd + 1 : 2 * hd + 2] + unit_eps)
    q_scale_row, k_scale_row = as_row(q_scale), as_row(k_scale)
    gram = jnp.where(same_head, fold(packed, fold_a, across), 0.0) * q_scale * k_scale_row
    grad_attn = jnp.where(same_head, fold(packed, fold_b, across), 0.0)
    head_of = lax.broadcasted_iota(jnp.int32, (ch, 1), 0) // hd
    sharp = jnp.zeros((ch, 1), F32)
    for h in range(heads):
        sharp = jnp.where(head_of == h, sharp_ref[h], sharp)
    powers = jnp.where(same_head, jnp.exp(sharp * gram), 0.0)
    attention = powers / jnp.sum(powers, axis=-1, keepdims=True)
    scores = attention * (grad_attn - jnp.sum(attention * grad_attn, axis=-1, keepdims=True))
    pixels = R * C * n0
    weighted = scores * gram
    per_channel = jnp.sum(weighted, axis=-1, keepdims=True)
    row_head = lax.broadcasted_iota(jnp.int32, (ch, LANES), 0) // hd
    sharp_out[...] = (
        jnp.sum(jnp.where(place_c == row_head, per_channel, 0.0), axis=0, keepdims=True) / pixels
    )
    q_dots = as_row(sharp * per_channel)
    k_dots = jnp.sum(sharp * weighted, axis=0, keepdims=True)
    blend = halves(q_scale * (sharp * scores) * k_scale_row)

    def keep(value, lo):
        value = jnp.where(mask1, value, 0.0).astype(BF16).astype(F32)
        grad_mixed[:, :, lo : lo + ch] = value.reshape(H + 2, W, ch)

    q_pair, k_pair, g_pair = [(split[2 * n], split[2 * n + 1]) for n in range(3)]
    q_wide = mixed[:, :, 0:ch].reshape(n1, ch)
    k_wide = mixed[:, :, ch : 2 * ch].reshape(n1, ch)
    keep(dot_split(k_pair, blend, across) - q_wide * (q_scale_row * q_scale_row * q_dots), 0)
    keep(dot_split(q_pair, blend) - k_wide * (k_scale_row * k_scale_row * k_dots), ch)
    keep(dot_split(g_pair, halves(attention)), 2 * ch)

    size2 = pay2.shape[0] // R
    used2 = 9 * (c3 // LANES)
    pay2[used2:, :] = jnp.zeros((R * size2 - used2, LANES), F32)
    own_cols = lax.broadcasted_iota(jnp.int32, (W, LANES), 0) < B
    strips = W // 8

    @pl.loop(0, c3 // LANES)
    def _(n):
        lanes = lanes_of(n)

        def body(i, sums):
            mid = jnp.where(own_cols, grad_mixed[i + 1, :, lanes], 0.0)
            moved = [pltpu.roll(mid, W - 1, 0), mid, pltpu.roll(mid, 1, 0)]
            new = []
            for a in range(3):
                window = qkv[i + 1 + a, :, lanes]
                for b in range(3):
                    term = (window * moved[b]).reshape(strips, 8, LANES)
                    new.append(sums[3 * a + b] + jnp.sum(term, axis=0))
            return tuple(new)

        sums = tuple(jnp.zeros((8, LANES), F32) for _ in range(9))
        sums = lax.fori_loop(0, H, body, sums, unroll=True)
        for t in range(9):
            pay2[pl.ds(n * 9 + t, 1), :] = jnp.sum(sums[t], axis=0, keepdims=True)

    pay2_parts = pay2.reshape(R, size2, LANES)
    scatter(3, pay2_parts, part2)

    @pl.loop(0, c3 // LANES)
    def _(n):
        lanes = lanes_of(n)
        taps = tap_rows(lanes)
        for i in range(H):
            grads = [grad_mixed[i + 2 - a, :, lanes] for a in range(3)]
            s = [sum(taps[a][b] * grads[a] for a in range(3)) for b in range(3)]
            value = s[1] + pltpu.roll(s[0], W - 1, 0) + pltpu.roll(s[2], 1, 0)
            grad_qkv[i, :, lanes] = value[0:B, :].astype(BF16)

    to_cols(4, cols2, scattered(3, pay2_parts, part2))

    grad_normed = dot_bf16(grad_qkv[...].reshape(n0, c3), proj_ref[...], across)
    standard = standard_ref[...]
    gain_sum = jnp.sum(grad_normed * standard, axis=0, keepdims=True)
    gain_rows = [gain_sum[:, n * LANES : (n + 1) * LANES] for n in range(ch // LANES)]
    gain_rows += [jnp.zeros((gain_all.shape[1] - len(gain_rows), LANES), F32)]
    to_rows(5, gain_all, jnp.concatenate(gain_rows, 0))
    to_rows(6, full2, summed(4, cols2, C))

    scaled = grad_normed * gain_ref[...]
    slope = jnp.mean(scaled * standard, axis=-1, keepdims=True)
    grad_input = inv_ref[:, 0:1] * (
        scaled - jnp.mean(scaled, axis=-1, keepdims=True) - standard * slope
    )
    out_ref[...] = (u_ref[...].astype(F32) + grad_input.reshape(H, B, ch)).astype(BF16)
    store = pltpu.make_async_copy(out_ref, out_hbm, load_sem.at[6])
    store.start()

    to_cols(7, gain_cols, summed(5, gain_all, R))
    arrive(6, full2, R - 1)
    flat = full2[...].reshape(R * size2, LANES) / pixels
    for n in range(c3 // LANES):
        taps_out[:, n * LANES : (n + 1) * LANES] = flat[n * 9 : n * 9 + 9, :]
    gain_total = summed(7, gain_cols, C) / pixels
    for n in range(ch // LANES):
        gain_out[:, n * LANES : (n + 1) * LANES] = gain_total[n : n + 1, :]
    store.wait()
    for n, buf in enumerate((col_in, corner_in, row_x, row_u)):
        halo_copy(n, buf).wait_send()
    sent = (
        (0, part1, R),
        (1, cols1, C),
        (2, full1, R),
        (3, part2, R),
        (4, cols2, C),
        (5, gain_all, R),
        (6, full2, R),
        (7, gain_cols, C),
    )
    for phase, buf, count in sent:
        left_here(phase, buf, count - 1)


def pay_rows(value, rows):
    if rows == value.shape[0]:
        return value
    fill = jnp.zeros((rows - value.shape[0], value.shape[1]), value.dtype)
    return jnp.concatenate([value, fill], axis=0)


def local(R, C, x, u, gain, proj, taps, sharp, final):
    H, B, ch = x.shape
    heads = sharp.shape[0]
    c3 = 3 * ch
    W = B + 8
    size1 = ceil_to(-(-ch // R), 8)
    rows2 = 9 * (c3 // LANES)
    S = W - B
    size3 = ceil_to(ch // LANES, 8)
    size2 = ceil_to(-(-rows2 // R), 8)
    vmem = pl.BlockSpec(memory_space=pltpu.VMEM)
    hbm = pl.BlockSpec(memory_space=pltpu.HBM)
    DMA = pltpu.SemaphoreType.DMA
    out, gain_sum, taps_sum, sharp_sum = pl.pallas_call(
        functools.partial(kernel, (R, C, H, B, ch, heads)),
        name="attention_backward",
        out_shape=(
            jax.ShapeDtypeStruct((H, B, ch), BF16),
            jax.ShapeDtypeStruct((1, ch), F32),
            jax.ShapeDtypeStruct((9, c3), F32),
            jax.ShapeDtypeStruct((1, LANES), F32),
        ),
        in_specs=[hbm] * 5 + [pl.BlockSpec(memory_space=pltpu.SMEM), hbm],
        out_specs=[hbm] + [vmem] * 3,
        scratch_shapes=[
            pltpu.VMEM((H, B, ch), BF16),
            pltpu.VMEM((H, B, ch), BF16),
            pltpu.VMEM((1, ch), F32),
            pltpu.VMEM((ch, c3), BF16),
            pltpu.VMEM((3, 3, c3), BF16),
            pltpu.VMEM((ch, ch), BF16),
            pltpu.VMEM((H, B, ch), BF16),
            DMA((7,)),
            pltpu.VMEM((2, H, 4, ch), F32),
            pltpu.VMEM((2, H, 4, ch), F32),
            pltpu.VMEM((2, 2, 2, 4, ch), F32),
            pltpu.VMEM((2, 2, B, ch), BF16),
            pltpu.VMEM((2, 1, B, ch), BF16),
            pltpu.VMEM((4, W, ch), F32),
            pltpu.VMEM((H, S, ch), F32),
            pltpu.VMEM((2, W, ch), F32),
            pltpu.VMEM((H, S, ch), F32),
            pltpu.VMEM((H * B, ch), F32),
            pltpu.VMEM((H * B, LANES), F32),
            pltpu.VMEM((H + 4, W, c3), F32),
            pltpu.VMEM((H + 2, W, c3), F32),
            pltpu.VMEM((H + 2, W, ch), F32),
            pltpu.VMEM((H + 2, W, c3), F32),
            pltpu.VMEM((H, B, c3), BF16),
            pltpu.VMEM((6, (H + 2) * W, ch), BF16),
            pltpu.VMEM((R, size1, LANES), F32),
            pltpu.VMEM((R - 1, size1, LANES), F32),
            pltpu.VMEM((C, size1, LANES), F32),
            pltpu.VMEM((R, size1, LANES), F32),
            pltpu.VMEM((R * size2, LANES), F32),
            pltpu.VMEM((R - 1, size2, LANES), F32),
            pltpu.VMEM((C, size2, LANES), F32),
            pltpu.VMEM((R, size2, LANES), F32),
            pltpu.VMEM((R, size3, LANES), F32),
            pltpu.VMEM((C, size3, LANES), F32),
            DMA((4,)),
            DMA((4,)),
            DMA((8,)),
            DMA((8,)),
        ],
        compiler_params=pltpu.CompilerParams(
            collective_id=0, has_side_effects=True, vmem_limit_bytes=56203673
        ),
    )(x, u, gain, proj, taps, sharp, final)
    return (out, gain_sum.reshape(ch), taps_sum.reshape(3, 3, c3), sharp_sum[0, :heads])


def solution(mesh):
    R, C = mesh.shape["rows"], mesh.shape["cols"]
    return jax.shard_map(
        functools.partial(local, R, C),
        mesh=mesh,
        in_specs=(P("rows", "cols", None), P("rows", "cols", None), P(), P(), P(), P(), P()),
        out_specs=(P("rows", "cols", None), P(), P(), P()),
        check_vma=False,
    )
```

```python
import functools

import jax
import jax.numpy as jnp
from jax import lax
from jax.experimental import pallas as pl
from jax.experimental.pallas import tpu as pltpu
from jax.sharding import PartitionSpec as P

norm_eps = 1e-05
unit_eps = 1e-06
F32 = jnp.float32
BF16 = jnp.bfloat16
LANES = 128


def dot_bf16(a, b, dims=((1,), (0,))):
    return lax.dot_general(a, b, (dims, ((), ())), preferred_element_type=F32)


def ceil_to(value, step):
    return (value + step - 1) // step * step


def halves(a):
    high = a.astype(BF16)
    return high, (a - high.astype(F32)).astype(BF16)


def dot_split(a, b, dims=((1,), (0,))):
    return dot_bf16(a[0], b[0], dims) + (dot_bf16(a[0], b[1], dims) + dot_bf16(a[1], b[0], dims))


def kernel(
    geo,
    x_hbm,
    u_hbm,
    gain_hbm,
    proj_hbm,
    taps_hbm,
    sharp_ref,
    final_hbm,
    out_hbm,
    gain_out,
    taps_out,
    sharp_out,
    x_ref,
    u_ref,
    gain_ref,
    proj_ref,
    taps_ref,
    final_ref,
    out_ref,
    load_sem,
    stage,
    col_in,
    corner_in,
    row_x,
    row_u,
    rim_x,
    side_x,
    rim_u,
    side_u,
    standard_ref,
    inv_ref,
    qkv,
    mixed,
    grad_out,
    grad_mixed,
    grad_qkv,
    split,
    pay1,
    part1,
    cols1,
    full1,
    pay2,
    part2,
    cols2,
    full2,
    gain_all,
    gain_cols,
    halo_send,
    halo_recv,
    red_send,
    red_recv,
):
    R, C, H, B, ch, heads = geo
    hd = ch // heads
    c3 = 3 * ch
    W = B + 8
    S = W - B
    row = lax.axis_index("rows")
    col = lax.axis_index("cols")
    up, down = lax.rem(row + R - 1, R), lax.rem(row + 1, R)
    left, right = lax.rem(col + C - 1, C), lax.rem(col + 1, C)
    MESH = pl.DeviceIdType.MESH

    barrier = pltpu.get_barrier_semaphore()

    def greet(r, c):
        pl.semaphore_signal(barrier, inc=1, device_id=(r, c), device_id_type=MESH)

    for i in range(1, R):
        greet(lax.rem(row + i, R), col)
    for i in range(1, C):
        greet(row, lax.rem(col + i, C))
    for r in (up, down):
        for c in (left, right):
            greet(r, c)

    loads = [
        pltpu.make_async_copy(src, dst, load_sem.at[n])
        for n, (src, dst) in enumerate(
            (
                (x_hbm, x_ref),
                (u_hbm, u_ref),
                (gain_hbm, gain_ref.at[0]),
                (proj_hbm, proj_ref),
                (final_hbm, final_ref),
                (taps_hbm, taps_ref),
            )
        )
    ]
    for load in loads:
        load.start()
    loads[0].wait()
    loads[1].wait()
    xf = x_ref[...].astype(F32)
    uf = u_ref[...].astype(F32)
    stage[0, :, 0:2, :] = xf[:, 0:2, :]
    stage[0, :, 2:3, :] = uf[:, 0:1, :]
    stage[0, :, 3:4, :] = uf[:, 0:1, :]
    stage[1, :, 0:2, :] = xf[:, B - 2 : B, :]
    stage[1, :, 2:3, :] = uf[:, B - 1 : B, :]
    stage[1, :, 3:4, :] = uf[:, B - 1 : B, :]

    pl.semaphore_wait(barrier, (R - 1) + (C - 1) + 4)

    def send(n, src, dst, r, c):
        pltpu.make_async_remote_copy(
            src_ref=src,
            dst_ref=dst,
            send_sem=halo_send.at[n],
            recv_sem=halo_recv.at[n],
            device_id=(r, c),
            device_id_type=MESH,
        ).start()

    send(0, stage.at[0], col_in.at[1], row, left)
    send(0, stage.at[1], col_in.at[0], row, right)
    send(1, stage.at[0, pl.ds(0, 2)], corner_in.at[1, 1], up, left)
    send(1, stage.at[1, pl.ds(0, 2)], corner_in.at[1, 0], up, right)
    send(1, stage.at[0, pl.ds(H - 2, 2)], corner_in.at[0, 1], down, left)
    send(1, stage.at[1, pl.ds(H - 2, 2)], corner_in.at[0, 0], down, right)
    send(2, x_ref.at[pl.ds(0, 2)], row_x.at[1], up, col)
    send(2, x_ref.at[pl.ds(H - 2, 2)], row_x.at[0], down, col)
    send(3, u_ref.at[pl.ds(0, 1)], row_u.at[1], up, col)
    send(3, u_ref.at[pl.ds(H - 1, 1)], row_u.at[0], down, col)

    def halo_copy(n, buf):
        return pltpu.make_async_remote_copy(
            src_ref=buf,
            dst_ref=buf,
            send_sem=halo_send.at[n],
            recv_sem=halo_recv.at[n],
            device_id=(row, left),
            device_id_type=MESH,
        )

    n0 = H * B
    across = ((1,), (1,))

    def normalise(feat):
        centred = feat - jnp.mean(feat, axis=-1, keepdims=True)
        inv_std = lax.rsqrt(jnp.mean(centred * centred, axis=-1, keepdims=True) + norm_eps)
        return centred * inv_std, inv_std

    def project(normed):
        return dot_bf16(normed.astype(BF16), proj_ref[...]).astype(BF16).astype(F32)

    loads[2].wait()
    loads[3].wait()
    standard, inv_std = normalise(xf.reshape(n0, ch))
    standard_ref[...] = standard
    inv_ref[...] = jnp.broadcast_to(inv_std, (n0, LANES))
    qkv[2 : H + 2, 0:B, :] = project(standard * gain_ref[...]).reshape(H, B, c3)
    loads[4].wait()
    loads[5].wait()
    grad_out[1 : H + 1, 0:B, :] = dot_bf16(
        u_ref[...].reshape(n0, ch), final_ref[...], across
    ).reshape(H, B, ch)

    rim_x[:, B:W, :] = jnp.zeros((4, S, ch), F32)
    side_x[...] = jnp.zeros((H, S, ch), F32)
    rim_u[:, B:W, :] = jnp.zeros((2, S, ch), F32)
    side_u[...] = jnp.zeros((H, S, ch), F32)
    halo_copy(0, col_in).wait_recv()
    halo_copy(1, corner_in).wait_recv()
    halo_copy(2, row_x).wait_recv()
    halo_copy(3, row_u).wait_recv()
    side_x[:, 0:2, :] = col_in[1, :, 0:2, :]
    side_x[:, S - 2 : S, :] = col_in[0, :, 0:2, :]
    for v in (0, 1):
        at = 2 * v
        rim_x[at : at + 2, 0:B, :] = row_x[v].astype(F32)
        rim_x[at : at + 2, B : B + 2, :] = corner_in[v, 1, :, 0:2, :]
        rim_x[at : at + 2, W - 2 : W, :] = corner_in[v, 0, :, 0:2, :]

    def inside(shape, i, first_col, width):
        j = first_col + lax.broadcasted_iota(jnp.int32, shape, 1)
        rim_right = (j >= B) & (j < B + width) & (col < C - 1)
        rim_left = (j >= W - width) & (col > 0)
        ok = (i >= 0) & (i < R * H) & ((j < B) | rim_right | rim_left)
        return jnp.where(ok, 1.0, 0.0).astype(F32).reshape(-1, LANES)[:, 0:1] > 0.5

    def plane(shape):
        return lax.broadcasted_iota(jnp.int32, shape, 0)

    n_rim, n_side = 4 * W, H * S
    plane4 = plane((4, W, LANES))
    rim_rows = row * H + jnp.where(plane4 < 2, plane4 - 2, plane4 + H - 2)
    rim_ok = inside((4, W, LANES), rim_rows, 0, 2)
    side_ok = inside((H, S, LANES), row * H + plane((H, S, LANES)), B, 2)
    rim_norm = normalise(rim_x[...].reshape(n_rim, ch))[0] * gain_ref[...]
    side_norm = normalise(side_x[...].reshape(n_side, ch))[0] * gain_ref[...]
    rim_qkv = project(
        jnp.concatenate([jnp.where(rim_ok, rim_norm, 0.0), jnp.where(side_ok, side_norm, 0.0)], 0)
    )
    qkv[0:2, :, :] = rim_qkv[0 : 2 * W].reshape(2, W, c3)
    qkv[H + 2 : H + 4, :, :] = rim_qkv[2 * W : n_rim].reshape(2, W, c3)
    qkv[2 : H + 2, B:W, :] = rim_qkv[n_rim:].reshape(H, S, c3)

    def tap_rows(lanes):
        return [
            [taps_ref[a, :, lanes].astype(F32)[b : b + 1, :] for b in range(3)] for a in range(3)
        ]

    def lanes_of(n):
        return pl.ds(pl.multiple_of(n * LANES, LANES), LANES)

    def mix(taps, lanes, i):
        window = [qkv[i + a, :, lanes] for a in range(3)]
        t = [sum(taps[a][b] * window[a] for a in range(3)) for b in range(3)]
        mixed[i, :, lanes] = t[1] + pltpu.roll(t[0], 1, 0) + pltpu.roll(t[2], W - 1, 0)

    @pl.loop(0, c3 // LANES)
    def _(n):
        taps = tap_rows(lanes_of(n))
        for i in range(1, H + 1):
            mix(taps, lanes_of(n), i)

    def own(lo):
        return mixed[1 : H + 1, 0:B, lo : lo + ch].reshape(n0, ch)

    q, k, v = own(0), own(ch), own(2 * ch)
    g = grad_out[1 : H + 1, 0:B, :].reshape(n0, ch)
    head_r = lax.broadcasted_iota(jnp.int32, (ch, ch), 0) // hd
    head_c = lax.broadcasted_iota(jnp.int32, (ch, ch), 1) // hd
    same_head = head_r == head_c
    diagonal = lax.broadcasted_iota(jnp.int32, (ch, ch), 0) == lax.broadcasted_iota(
        jnp.int32, (ch, ch), 1
    )
    along = ((0,), (0,))

    def as_column(line):
        return jnp.sum(jnp.where(diagonal, line, 0.0), axis=1, keepdims=True)

    def as_row(column):
        return jnp.sum(jnp.where(diagonal, column, 0.0), axis=0, keepdims=True)

    raw_gram = jnp.where(same_head, dot_split(halves(q), halves(k), along), 0.0)
    raw_attn = jnp.where(same_head, dot_split(halves(g), halves(v), along), 0.0)
    q_squares = as_column(jnp.sum(q * q, axis=0, keepdims=True))
    k_squares = as_column(jnp.sum(k * k, axis=0, keepdims=True))
    place_r = lax.rem(lax.broadcasted_iota(jnp.int32, (ch, LANES), 0), hd)
    place_c = lax.broadcasted_iota(jnp.int32, (ch, LANES), 1)
    fold_a = jnp.where(place_r == place_c, 1.0, 0.0).astype(BF16)
    fold_b = jnp.where(place_r + hd == place_c, 1.0, 0.0).astype(BF16)

    def thirds(a):
        high, low = halves(a)
        return high, low, (a - high.astype(F32) - low.astype(F32)).astype(BF16)

    def fold(a, matrix, dims=((1,), (0,))):
        return sum(dot_bf16(part, matrix, dims) for part in thirds(a))

    packed = fold(raw_gram, fold_a) + fold(raw_attn, fold_b)
    packed = jnp.where(place_c == 2 * hd, q_squares, packed)
    packed = jnp.where(place_c == 2 * hd + 1, k_squares, packed)
    size1 = pay1.shape[1]
    pay1[...] = pay_rows(packed, R * size1).reshape(R, size1, LANES)

    def copy_to(phase, src, dst, r, c):
        return pltpu.make_async_remote_copy(
            src_ref=src,
            dst_ref=dst,
            send_sem=red_send.at[phase],
            recv_sem=red_recv.at[phase],
            device_id=(r, c),
            device_id_type=MESH,
        )

    def arrive(phase, buf, count):
        some = buf.at[pl.ds(0, count)]
        copy_to(phase, some, some, row, left).wait_recv()

    def left_here(phase, buf, count):
        some = buf.at[pl.ds(0, count)]
        copy_to(phase, some, some, row, left).wait_send()

    def scatter(phase, pay, part):
        for i in range(1, R):
            to = lax.rem(row + i, R)
            copy_to(phase, pay.at[to], part.at[i - 1], to, col).start()

    def scattered(phase, pay, part):
        arrive(phase, part, R - 1)
        total = pay[row]
        for i in range(R - 1):
            total = total + part[i]
        return total

    def to_cols(phase, cols, value):
        cols[col] = value
        for i in range(1, C):
            to = lax.rem(col + i, C)
            copy_to(phase, cols.at[col], cols.at[col], row, to).start()

    def summed(phase, buf, count):
        arrive(phase, buf, count - 1)
        total = buf[0]
        for i in range(1, count):
            total = total + buf[i]
        return total

    def to_rows(phase, full, value):
        full[row] = value
        for i in range(1, R):
            to = lax.rem(row + i, R)
            copy_to(phase, full.at[row], full.at[row], to, col).start()

    scatter(0, pay1, part1)

    @pl.loop(0, c3 // LANES)
    def _(n):
        taps = tap_rows(lanes_of(n))
        for i in (0, H + 1):
            mix(taps, lanes_of(n), i)

    side_u[:, 0:1, :] = col_in[1, :, 2:3, :]
    side_u[:, S - 1 : S, :] = col_in[0, :, 2:3, :]
    for v, near in ((0, 1), (1, 0)):
        rim_u[v : v + 1, 0:B, :] = row_u[v].astype(F32)
        rim_u[v : v + 1, B : B + 1, :] = corner_in[v, 1, near : near + 1, 2:3, :]
        rim_u[v : v + 1, W - 1 : W, :] = corner_in[v, 0, near : near + 1, 2:3, :]
    n1 = (H + 2) * W
    rows1 = row * H - 1 + plane((H + 2, W, LANES))
    mask1 = inside((H + 2, W, LANES), rows1, 0, 1)
    rim_adjoint = jnp.concatenate(
        [rim_u[...].reshape(2 * W, ch), side_u[...].reshape(n_side, ch)], 0
    ).astype(BF16)
    rim_out = dot_bf16(rim_adjoint, final_ref[...], across)
    grad_out[0:1, :, :] = rim_out[0:W].reshape(1, W, ch)
    grad_out[H + 1 : H + 2, :, :] = rim_out[W : 2 * W].reshape(1, W, ch)
    grad_out[1 : H + 1, B:W, :] = rim_out[2 * W :].reshape(H, S, ch)
    for n, wide in enumerate((mixed[:, :, 0:ch], mixed[:, :, ch : 2 * ch], grad_out[...])):
        split[2 * n], split[2 * n + 1] = halves(wide.reshape(n1, ch))

    to_cols(1, cols1, scattered(0, pay1, part1))
    to_rows(2, full1, summed(1, cols1, C))
    arrive(2, full1, R - 1)

    packed = full1[...].reshape(R * size1, LANES)[0:ch, :]
    q_scale = lax.rsqrt(packed[:, 2 * hd : 2 * hd + 1] + unit_eps)
    k_scale = lax.rsqrt(packed[:, 2 * hd + 1 : 2 * hd + 2] + unit_eps)
    q_scale_row, k_scale_row = as_row(q_scale), as_row(k_scale)
    gram = jnp.where(same_head, fold(packed, fold_a, across), 0.0) * q_scale * k_scale_row
    grad_attn = jnp.where(same_head, fold(packed, fold_b, across), 0.0)
    head_of = lax.broadcasted_iota(jnp.int32, (ch, 1), 0) // hd
    sharp = jnp.zeros((ch, 1), F32)
    for h in range(heads):
        sharp = jnp.where(head_of == h, sharp_ref[h], sharp)
    powers = jnp.where(same_head, jnp.exp(sharp * gram), 0.0)
    attention = powers / jnp.sum(powers, axis=-1, keepdims=True)
    scores = attention * (grad_attn - jnp.sum(attention * grad_attn, axis=-1, keepdims=True))
    pixels = R * C * n0
    weighted = scores * gram
    per_channel = jnp.sum(weighted, axis=-1, keepdims=True)
    row_head = lax.broadcasted_iota(jnp.int32, (ch, LANES), 0) // hd
    sharp_out[...] = (
        jnp.sum(jnp.where(place_c == row_head, per_channel, 0.0), axis=0, keepdims=True) / pixels
    )
    q_dots = as_row(sharp * per_channel)
    k_dots = jnp.sum(sharp * weighted, axis=0, keepdims=True)
    blend = halves(q_scale * (sharp * scores) * k_scale_row)

    def keep(value, lo):
        value = jnp.where(mask1, value, 0.0).astype(BF16).astype(F32)
        grad_mixed[:, :, lo : lo + ch] = value.reshape(H + 2, W, ch)

    q_pair, k_pair, g_pair = [(split[2 * n], split[2 * n + 1]) for n in range(3)]
    q_wide = mixed[:, :, 0:ch].reshape(n1, ch)
    k_wide = mixed[:, :, ch : 2 * ch].reshape(n1, ch)
    keep(dot_split(k_pair, blend, across) - q_wide * (q_scale_row * q_scale_row * q_dots), 0)
    keep(dot_split(q_pair, blend) - k_wide * (k_scale_row * k_scale_row * k_dots), ch)
    keep(dot_split(g_pair, halves(attention)), 2 * ch)

    size2 = pay2.shape[0] // R
    used2 = 9 * (c3 // LANES)
    pay2[used2:, :] = jnp.zeros((R * size2 - used2, LANES), F32)
    own_cols = lax.broadcasted_iota(jnp.int32, (W, LANES), 0) < B
    strips = W // 8

    @pl.loop(0, c3 // LANES)
    def _(n):
        lanes = lanes_of(n)

        def body(i, sums):
            mid = jnp.where(own_cols, grad_mixed[i + 1, :, lanes], 0.0)
            moved = [pltpu.roll(mid, W - 1, 0), mid, pltpu.roll(mid, 1, 0)]
            new = []
            for a in range(3):
                window = qkv[i + 1 + a, :, lanes]
                for b in range(3):
                    term = (window * moved[b]).reshape(strips, 8, LANES)
                    new.append(sums[3 * a + b] + jnp.sum(term, axis=0))
            return tuple(new)

        sums = tuple(jnp.zeros((8, LANES), F32) for _ in range(9))
        sums = lax.fori_loop(0, H, body, sums, unroll=True)
        for t in range(9):
            pay2[pl.ds(n * 9 + t, 1), :] = jnp.sum(sums[t], axis=0, keepdims=True)

    pay2_parts = pay2.reshape(R, size2, LANES)
    scatter(3, pay2_parts, part2)

    @pl.loop(0, c3 // LANES)
    def _(n):
        lanes = lanes_of(n)
        taps = tap_rows(lanes)
        for i in range(H):
            grads = [grad_mixed[i + 2 - a, :, lanes] for a in range(3)]
            s = [sum(taps[a][b] * grads[a] for a in range(3)) for b in range(3)]
            value = s[1] + pltpu.roll(s[0], W - 1, 0) + pltpu.roll(s[2], 1, 0)
            grad_qkv[i, :, lanes] = value[0:B, :].astype(BF16)

    to_cols(4, cols2, scattered(3, pay2_parts, part2))

    grad_normed = dot_bf16(grad_qkv[...].reshape(n0, c3), proj_ref[...], across)
    standard = standard_ref[...]
    gain_sum = jnp.sum(grad_normed * standard, axis=0, keepdims=True)
    gain_rows = [gain_sum[:, n * LANES : (n + 1) * LANES] for n in range(ch // LANES)]
    gain_rows += [jnp.zeros((gain_all.shape[1] - len(gain_rows), LANES), F32)]
    to_rows(5, gain_all, jnp.concatenate(gain_rows, 0))
    to_rows(6, full2, summed(4, cols2, C))

    scaled = grad_normed * gain_ref[...]
    slope = jnp.mean(scaled * standard, axis=-1, keepdims=True)
    grad_input = inv_ref[:, 0:1] * (
        scaled - jnp.mean(scaled, axis=-1, keepdims=True) - standard * slope
    )
    out_ref[...] = (u_ref[...].astype(F32) + grad_input.reshape(H, B, ch)).astype(BF16)
    store = pltpu.make_async_copy(out_ref, out_hbm, load_sem.at[6])
    store.start()

    to_cols(7, gain_cols, summed(5, gain_all, R))
    arrive(6, full2, R - 1)
    flat = full2[...].reshape(R * size2, LANES) / pixels
    for n in range(c3 // LANES):
        taps_out[:, n * LANES : (n + 1) * LANES] = flat[n * 9 : n * 9 + 9, :]
    gain_total = summed(7, gain_cols, C) / pixels
    for n in range(ch // LANES):
        gain_out[:, n * LANES : (n + 1) * LANES] = gain_total[n : n + 1, :]
    store.wait()
    for n, buf in enumerate((col_in, corner_in, row_x, row_u)):
        halo_copy(n, buf).wait_send()
    sent = (
        (0, part1, R),
        (1, cols1, C),
        (2, full1, R),
        (3, part2, R),
        (4, cols2, C),
        (5, gain_all, R),
        (6, full2, R),
        (7, gain_cols, C),
    )
    for phase, buf, count in sent:
        left_here(phase, buf, count - 1)


def pay_rows(value, rows):
    if rows == value.shape[0]:
        return value
    fill = jnp.zeros((rows - value.shape[0], value.shape[1]), value.dtype)
    return jnp.concatenate([value, fill], axis=0)


def pin(*arrays):
    return [pltpu.with_memory_space_constraint(a, pltpu.HBM) for a in arrays]


def local(R, C, x, u, gain, proj, taps, sharp, final):
    H, B, ch = x.shape
    heads = sharp.shape[0]
    c3 = 3 * ch
    W = B + 8
    size1 = ceil_to(-(-ch // R), 8)
    rows2 = 9 * (c3 // LANES)
    S = W - B
    size3 = ceil_to(ch // LANES, 8)
    size2 = ceil_to(-(-rows2 // R), 8)
    vmem = pl.BlockSpec(memory_space=pltpu.VMEM)
    hbm = pl.BlockSpec(memory_space=pltpu.HBM)
    DMA = pltpu.SemaphoreType.DMA
    out, gain_sum, taps_sum, sharp_sum = pl.pallas_call(
        functools.partial(kernel, (R, C, H, B, ch, heads)),
        name="attention_backward",
        out_shape=(
            jax.ShapeDtypeStruct((H, B, ch), BF16),
            jax.ShapeDtypeStruct((1, ch), F32),
            jax.ShapeDtypeStruct((9, c3), F32),
            jax.ShapeDtypeStruct((1, LANES), F32),
        ),
        in_specs=[hbm] * 5 + [pl.BlockSpec(memory_space=pltpu.SMEM), hbm],
        out_specs=[hbm] + [vmem] * 3,
        scratch_shapes=[
            pltpu.VMEM((H, B, ch), BF16),
            pltpu.VMEM((H, B, ch), BF16),
            pltpu.VMEM((1, ch), F32),
            pltpu.VMEM((ch, c3), BF16),
            pltpu.VMEM((3, 3, c3), BF16),
            pltpu.VMEM((ch, ch), BF16),
            pltpu.VMEM((H, B, ch), BF16),
            DMA((7,)),
            pltpu.VMEM((2, H, 4, ch), F32),
            pltpu.VMEM((2, H, 4, ch), F32),
            pltpu.VMEM((2, 2, 2, 4, ch), F32),
            pltpu.VMEM((2, 2, B, ch), BF16),
            pltpu.VMEM((2, 1, B, ch), BF16),
            pltpu.VMEM((4, W, ch), F32),
            pltpu.VMEM((H, S, ch), F32),
            pltpu.VMEM((2, W, ch), F32),
            pltpu.VMEM((H, S, ch), F32),
            pltpu.VMEM((H * B, ch), F32),
            pltpu.VMEM((H * B, LANES), F32),
            pltpu.VMEM((H + 4, W, c3), F32),
            pltpu.VMEM((H + 2, W, c3), F32),
            pltpu.VMEM((H + 2, W, ch), F32),
            pltpu.VMEM((H + 2, W, c3), F32),
            pltpu.VMEM((H, B, c3), BF16),
            pltpu.VMEM((6, (H + 2) * W, ch), BF16),
            pltpu.VMEM((R, size1, LANES), F32),
            pltpu.VMEM((R - 1, size1, LANES), F32),
            pltpu.VMEM((C, size1, LANES), F32),
            pltpu.VMEM((R, size1, LANES), F32),
            pltpu.VMEM((R * size2, LANES), F32),
            pltpu.VMEM((R - 1, size2, LANES), F32),
            pltpu.VMEM((C, size2, LANES), F32),
            pltpu.VMEM((R, size2, LANES), F32),
            pltpu.VMEM((R, size3, LANES), F32),
            pltpu.VMEM((C, size3, LANES), F32),
            DMA((4,)),
            DMA((4,)),
            DMA((8,)),
            DMA((8,)),
        ],
        compiler_params=pltpu.CompilerParams(
            collective_id=0, has_side_effects=True, vmem_limit_bytes=56203673
        ),
    )(*pin(x, u, gain, proj, taps), sharp, *pin(final))
    return (out, gain_sum.reshape(ch), taps_sum.reshape(3, 3, c3), sharp_sum[0, :heads])


def solution(mesh):
    R, C = mesh.shape["rows"], mesh.shape["cols"]
    return jax.shard_map(
        functools.partial(local, R, C),
        mesh=mesh,
        in_specs=(P("rows", "cols", None), P("rows", "cols", None), P(), P(), P(), P(), P()),
        out_specs=(P("rows", "cols", None), P(), P(), P()),
        check_vma=False,
    )
```
